1024 devices in a mesh: row: 4 (over x_lo, core), mesh: 256 (over y, z, x_hi).
Axes of the slice: x: 4 (x_hi: 2, x_lo: 2; x = x_hi * 2 + x_lo), y: 8, z: 16, core: 2. Of those that a mesh axis runs over, the one named last changes fastest.
Arguments:
- state: float32 [4, 7, 5, 8192, 256], P('row', None, None, 'mesh'), may hold values from -6 to 6
- inverse_blocks: float32 [4, 5, 5, 8192, 256], P('row', None, None, 'mesh'), may hold values from -0.25 to 0.5
- flux_jacobian: float32 [4, 5, 5], P('row'), may hold values from -2.5 to 2.5
- harmonics: int32 [4, 3], replicated, may hold values from 1 to 17, as said below
- interface_delay: float32 [4], replicated, may hold values from 0 to 1
- inflow: float32 [7, 5, 8192], P(None, None, 'mesh'), may hold values from -6 to 6
- pairing: int32 [4, 8192], P('row', 'mesh'), may hold values from 0 to 8191, as said below
Outputs:
- updated: float32 [4, 7, 5, 8192, 256], P('row', None, None, 'mesh')
The draws below stay inside these ranges and needn't reach their ends.
Inputs may be any that keep to these rules, and one draw needn't show every extreme that they name: `harmonics`: each row's harmonic numbers leave the remainders 1 to 3 in some order when divided by 7. `pairing`: within each aligned block of 32 lines, a permutation of that block's lines.
All inputs are finite; a program needn't handle non-finite values.
Results may differ from the reference program's by a relative error of at most 0.00016.
Values sent between devices are 32-bit elements; how exact they have to be, the bound alone decides.
No kernel may reach another device: no remote copies, remote signals or barrier semaphores. Data moves between devices by JAX's collectives and lax.ppermute only.
A program may use at most 32 MiB of HBM per device.

```python
import jax
import jax.numpy as jnp
from jax import lax

HARMONICS = 3
TIME_SAMPLES = 7
VARIABLES = 5
SECTIONS = 3
LINE_CELLS = 256
LINES_DEV = 32
LINES = 8192
BLADE_ROWS = 4


def draw_harmonics(key, part):
    split_keys = jax.random.split(key, 2)
    scores = jax.random.randint(split_keys[0], (BLADE_ROWS, HARMONICS), 0, 1 << 20) * HARMONICS + jnp.arange(HARMONICS, dtype=jnp.int32)[None, :]
    remainders = jnp.argsort(scores, axis=1).astype(jnp.int32) + 1
    multiples = jax.random.randint(split_keys[1], (BLADE_ROWS, HARMONICS), 0, 3).astype(jnp.int32)
    first_row = jnp.where(remainders[0] == HARMONICS, 2, jnp.where(remainders[0] == 1, 0, multiples[0])).astype(jnp.int32)
    multiples = multiples.at[0].set(first_row)
    return (remainders + TIME_SAMPLES * multiples).astype(jnp.int32)


def draw_pairing(key, part):
    block_count = LINES // LINES_DEV
    scores = jax.random.randint(key, (BLADE_ROWS, block_count, LINES_DEV), 0, 1 << 20) * LINES_DEV + jnp.arange(LINES_DEV, dtype=jnp.int32)[None, None, :]
    ordering = jnp.argsort(scores, axis=2).astype(jnp.int32)
    ordering = ordering + (jnp.arange(block_count, dtype=jnp.int32) * LINES_DEV)[None, :, None]
    return ordering.reshape(BLADE_ROWS, LINES).astype(jnp.int32)


def draw_inverse_blocks(key, part):
    split_keys = jax.random.split(key, 2)
    shape_diag = (BLADE_ROWS, VARIABLES, LINES, LINE_CELLS)
    shape_full = (BLADE_ROWS, VARIABLES, VARIABLES, LINES, LINE_CELLS)
    diagonal_part = jnp.exp(jax.random.uniform(split_keys[0], shape_diag, jnp.float32, jnp.log(0.15), jnp.log(0.45)))
    off_diagonal = jnp.clip(jax.random.normal(split_keys[1], shape_full, jnp.float32), -4.0, 4.0) * 0.06
    identity_mask = jnp.eye(VARIABLES, dtype=jnp.float32)[None, :, :, None, None]
    return (identity_mask * diagonal_part[:, :, None, :, :] + (1.0 - identity_mask) * off_diagonal).astype(jnp.float32)


def levels(key, dims, shards, smallest, top_value):
    loudness = 1.0
    for axis_at, shards_of in shards:
        steps = jax.random.uniform(jax.random.fold_in(jax.random.fold_in(key, 6), axis_at), (shards_of,), jnp.float32, smallest / len(shards), top_value / len(shards))
        loudness = loudness * jnp.repeat(jnp.exp(steps), dims[axis_at] // shards_of).reshape((-1,) + (1,) * (len(dims) - 1 - axis_at))
    return loudness


def bell_draw(rng, shape, spread, reach, cuts=(), kind=jnp.bfloat16):
    values = spread * jax.random.normal(rng, shape, jnp.float32)
    if cuts:
        values = values * levels(rng, shape, cuts, -0.22, 0.18)
    return jnp.clip(values, -reach, reach).astype(kind)


def setup_inputs(seed: int = 0) -> dict:
    keys = jax.random.split(jax.random.key(seed), 8)
    state = bell_draw(keys[0], (BLADE_ROWS, TIME_SAMPLES, VARIABLES, LINES, LINE_CELLS), 1.0, 6.0, ((0, 4), (3, 256)), jnp.float32)
    inverse_blocks = draw_inverse_blocks(jax.random.fold_in(keys[7], 71), 0)
    flux_jacobian = bell_draw(keys[2], (BLADE_ROWS, VARIABLES, VARIABLES), VARIABLES ** -0.5, 2.5, ((0, 4),), jnp.float32)
    harmonics = draw_harmonics(jax.random.fold_in(keys[7], 71), 0)
    interface_delay = jnp.clip(jax.random.uniform(keys[4], (BLADE_ROWS,), jnp.float32, 0.0, 1.0), 0.0, 1.0)
    inflow = bell_draw(keys[5], (TIME_SAMPLES, VARIABLES, LINES), 1.0, 6.0, ((2, 256),), jnp.float32)
    pairing = draw_pairing(jax.random.fold_in(keys[7], 71), 0)
    return {"state": state, "inverse_blocks": inverse_blocks, "flux_jacobian": flux_jacobian, "harmonics": harmonics, "interface_delay": interface_delay, "inflow": inflow, "pairing": pairing}


largest_mode = lax.Precision.HIGHEST
nu_second = 0.25
nu_fourth = 0.03
time_scale = 0.05


def spectral_basis(sample_times, harmonic_modes):
    phase_angles = 2.0 * jnp.pi * sample_times[:, None] * harmonic_modes[None, :].astype(jnp.float32)
    column_of_ones = jnp.ones((sample_times.shape[0], 1), jnp.float32)
    return jnp.concatenate([column_of_ones, jnp.cos(phase_angles), jnp.sin(phase_angles)], axis=1)


def basis_derivative(sample_times, harmonic_modes):
    angular_speeds = 2.0 * jnp.pi * harmonic_modes.astype(jnp.float32)
    phase_angles = sample_times[:, None] * angular_speeds[None, :]
    column_of_zeros = jnp.zeros((sample_times.shape[0], 1), jnp.float32)
    return jnp.concatenate([column_of_zeros, -angular_speeds[None, :] * jnp.sin(phase_angles), angular_speeds[None, :] * jnp.cos(phase_angles)], axis=1)


def forward_transform(sample_times, harmonic_modes):
    sample_count = sample_times.shape[0]
    mode_weights = jnp.concatenate([jnp.full((1,), 1.0 / sample_count, jnp.float32), jnp.full((sample_count - 1,), 2.0 / sample_count, jnp.float32)])
    return mode_weights[:, None] * spectral_basis(sample_times, harmonic_modes).T


def row_operators(harmonics, interface_delay, blade_row_index):
    sample_times = jnp.arange(TIME_SAMPLES, dtype=jnp.float32) / TIME_SAMPLES
    local_modes = harmonics[blade_row_index]
    upstream_modes = harmonics[jnp.maximum(blade_row_index - 1, 0)]
    spectral_derivative = jnp.dot(basis_derivative(sample_times, local_modes), forward_transform(sample_times, local_modes), precision=largest_mode, preferred_element_type=jnp.float32)
    interface_mapping = jnp.dot(spectral_basis(sample_times + interface_delay[blade_row_index], upstream_modes), forward_transform(sample_times, upstream_modes), precision=largest_mode, preferred_element_type=jnp.float32)
    return spectral_derivative, interface_mapping


def section_residual(padded, ghost_cells, spectral_derivative, flux_jac):
    centre = padded[:, :, 2:-2]
    before = jnp.concatenate([ghost_cells[:, :, :, None], centre[:, :, :, :-1]], axis=3)
    advection = jnp.einsum('ab,tbwl->tawl', flux_jac, centre - before, precision=largest_mode)
    second_diff = padded[:, :, 3:-1] - 2.0 * centre + padded[:, :, 1:-3]
    fourth_diff = padded[:, :, 4:] - 4.0 * padded[:, :, 3:-1] + 6.0 * centre - 4.0 * padded[:, :, 1:-3] + padded[:, :, :-4]
    temporal = jnp.einsum('ts,svwl->tvwl', spectral_derivative, centre, precision=largest_mode)
    return advection - nu_second * second_diff + nu_fourth * fourth_diff + time_scale * temporal


def apply_block(inverse, residual):
    total = inverse[None, :, 0] * residual[:, 0][:, None]
    for column_index in range(1, inverse.shape[1]):
        total = total + inverse[None, :, column_index] * residual[:, column_index][:, None]
    return total


def reference(state, inverse_blocks, flux_jacobian, harmonics, interface_delay, inflow, pairing):
    outlet = state[:, :, :, :, -1]
    results = []
    for blade_row_index in range(BLADE_ROWS):
        spectral_derivative, interface_mapping = row_operators(harmonics, interface_delay, blade_row_index)
        upstream = inflow if blade_row_index == 0 else outlet[blade_row_index - 1]
        paired = jnp.take(upstream, pairing[blade_row_index], axis=2)
        ghost_cells = jnp.einsum('ts,svw->tvw', interface_mapping, paired, precision=largest_mode)
        base_state = state[blade_row_index]
        current = base_state
        for section_index in range(SECTIONS):
            padded = jnp.pad(current, ((0, 0), (0, 0), (2, 2), (0, 0)))
            residual = section_residual(padded, ghost_cells, spectral_derivative, flux_jacobian[blade_row_index])
            section_weight = (section_index + 1.0) / SECTIONS
            current = base_state - section_weight * apply_block(inverse_blocks[blade_row_index], residual)
        results.append(current)
    return jnp.stack(results)
```

```python
import math

import jax
import jax.numpy as jnp
from jax import lax
from jax.experimental import pallas as pl
from jax.experimental.pallas import tpu as pltpu
from jax.sharding import PartitionSpec as P


TIMES = 7
VARS = 5
TV = TIMES * VARS
VV = VARS * VARS
SECTIONS = 3
LANES = 128
HALVES = 2
DEEP = 6
NEAR = 4
LINES = 32
S_ROWS = HALVES * TV * DEEP
I_ROWS = HALVES * VV * NEAR
MSG = S_ROWS + I_ROWS + NEAR

nu_second = 0.25
nu_fourth = 0.03
time_scale = 0.05

COS7 = [math.cos(2.0 * math.pi * k / 7.0) for k in range(7)]
SIN7 = [math.sin(2.0 * math.pi * k / 7.0) for k in range(7)]


def pick(table, index):
    value = jnp.float32(table[0])
    for k in range(1, 7):
        value = jnp.where(index == k, jnp.float32(table[k]), value)
    return value


def pack_message(out, s_ref, i_ref, s_from, i_from):
    for h in range(HALVES):
        cut = pl.ds(h * LANES, LANES)
        for k in range(TV):
            out[pl.ds((h * TV + k) * DEEP, DEEP), :] = s_ref[k, pl.ds(s_from, DEEP), cut]
        for k in range(VV):
            out[pl.ds(S_ROWS + (h * VV + k) * NEAR, NEAR), :] = i_ref[k, pl.ds(i_from, NEAR), cut]


def pack_kernel(pair_ref, state, inverse, inflow, up, outlet, s_hi, i_hi, last, flow, turned, sems):
    copies = [
        pltpu.make_async_copy(state.at[:, pl.ds(LINES - 8, 8), :], s_hi, sems.at[0]),
        pltpu.make_async_copy(inverse.at[:, pl.ds(LINES - 8, 8), :], i_hi, sems.at[1]),
        pltpu.make_async_copy(state.at[:, :, pl.ds(LANES, LANES)], last, sems.at[2]),
    ]
    for copy in copies:
        copy.start()
    copies[0].wait()
    copies[1].wait()
    pack_message(up, s_hi, i_hi, 8 - DEEP, 8 - NEAR)
    start_line = lax.axis_index("mesh") * LINES
    for j in range(NEAR):
        pair = (pair_ref[0, LINES - NEAR + j] - start_line).astype(jnp.float32)
        up[pl.ds(S_ROWS + I_ROWS + j, 1), :] = jnp.full((1, LANES), pair, jnp.float32)
    copies[2].wait()
    lane = lax.broadcasted_iota(jnp.int32, (LINES, LANES), 1)
    total = jnp.zeros((LINES, LANES), jnp.float32)
    for k in range(TV):
        total = jnp.where(lane == k, pltpu.roll(last[k], k + 1, 1), total)
    outlet[...] = total

    @pl.when(lax.axis_index("row") == lax.axis_size("row") - 1)
    def _():
        copy = pltpu.make_async_copy(inflow, flow, sems.at[3])
        copy.start()
        turned[...] = jnp.zeros((LANES, LANES), jnp.float32)
        copy.wait()
        for t in range(TIMES):
            for v in range(VARS):
                turned[pl.ds(t * VARS + v, 1), pl.ds(0, LINES)] = flow[v, pl.ds(t, 1), :]
        outlet[...] = jnp.transpose(turned[...])[:LINES, :]


F32 = jnp.float32
SMEM = pl.BlockSpec(memory_space=pltpu.SMEM)
VMEM = pl.BlockSpec(memory_space=pltpu.VMEM)
HBM = pl.BlockSpec(memory_space=pltpu.HBM)


def pack(pairing, state, inverse, inflow):
    return pl.pallas_call(
        pack_kernel,
        out_shape=(
            jax.ShapeDtypeStruct((MSG, LANES), F32),
            jax.ShapeDtypeStruct((LINES, LANES), F32),
        ),
        in_specs=[SMEM, HBM, HBM, HBM],
        out_specs=[VMEM] * 2,
        scratch_shapes=[
            pltpu.VMEM((TV, 8, HALVES * LANES), F32),
            pltpu.VMEM((VV, 8, HALVES * LANES), F32),
            pltpu.VMEM((TV, LINES, LANES), F32),
            pltpu.VMEM((VARS, TIMES, LINES), F32),
            pltpu.VMEM((LANES, LANES), F32),
            pltpu.SemaphoreType.DMA((4,)),
        ],
        name="pack",
        compiler_params=pltpu.CompilerParams(vmem_limit_bytes=4 << 20),
        cost_estimate=pl.CostEstimate(flops=10000, bytes_accessed=1_500_000, transcendentals=0),
    )(pairing, state, inverse, inflow)


def section_weights(flux, spectral, weight):
    w = jnp.float32(weight)
    scaled = [[flux[0, a, b] * w for b in range(VARS)] for a in range(VARS)]
    return scaled, [d * w for d in spectral]


def block_update(src, base, inv, ghost, r0, scaled, spectral, weight, emit):
    first = lax.broadcasted_iota(jnp.int32, (8, LANES), 1) == 0
    centre_c = jnp.float32((2.0 * nu_second + 6.0 * nu_fourth) * weight)
    near_c = jnp.float32((-nu_second - 4.0 * nu_fourth) * weight)
    far_c = jnp.float32(nu_fourth * weight)
    for h in range(HALVES):
        for t in range(TIMES):
            diffs = []
            for v in range(VARS):
                k = t * VARS + v
                here = src[h * TV + k, pl.ds(r0, 8), :]
                turned = pltpu.roll(here, 1, 1)
                if h == 0:
                    edge = ghost[k, pl.ds(r0, 8), :]
                else:
                    edge = pltpu.roll(src[k, pl.ds(r0, 8), :], 1, 1)
                diffs.append(here - jnp.where(first, edge, turned))
            residual = []
            for v in range(VARS):
                p = h * TV + t * VARS + v
                here = src[p, pl.ds(r0, 8), :]
                near = src[p, pl.ds(r0 - 1, 8), :] + src[p, pl.ds(r0 + 1, 8), :]
                far = src[p, pl.ds(r0 - 2, 8), :] + src[p, pl.ds(r0 + 2, 8), :]
                value = centre_c * here + near_c * near + far_c * far
                for j in range(1, 4):
                    early = src[h * TV + ((t - j) % TIMES) * VARS + v, pl.ds(r0, 8), :]
                    late = src[h * TV + ((t + j) % TIMES) * VARS + v, pl.ds(r0, 8), :]
                    value = value + spectral[j - 1] * (early - late)
                for b in range(VARS):
                    value = value + scaled[v][b] * diffs[b]
                residual.append(value)
            for v in range(VARS):
                p = h * TV + t * VARS + v
                value = base[p, pl.ds(r0, 8), :]
                for b in range(VARS):
                    value = value - inv[h * VV + v * VARS + b, pl.ds(r0, 8), :] * residual[b]
                emit(h, t * VARS + v, value)


def transfer_weights(modes_ref, delay_ref):
    row = lax.axis_index("row")
    upstream = jnp.maximum(row - 1, 0)
    delay = delay_ref[row]
    waves = []
    for j in range(3):
        mode = modes_ref[upstream, j]
        phase = jnp.full((8, LANES), mode.astype(jnp.float32) * delay, jnp.float32)
        phase = (phase - jnp.round(phase)) * jnp.float32(2.0 * math.pi)
        waves.append((lax.rem(mode, 7), jnp.cos(phase), jnp.sin(phase)))
    weights = []
    for d in range(TIMES):
        weight = jnp.full((8, LANES), 1.0 / 7.0, jnp.float32)
        for rest, cosine, sine in waves:
            index = lax.rem(rest * d, 7)
            weight = weight + jnp.float32(2.0 / 7.0) * (cosine * pick(COS7, index) - sine * pick(SIN7, index))
        weights.append(weight)
    return weights


def transfer(paired, weights):
    doubled = paired + pltpu.roll(paired, TV, 1)
    total = weights[0] * doubled
    for d in range(1, TIMES):
        total = total + weights[d] * pltpu.roll(doubled, VARS * d, 1)
    return total


def to_lane_zero(values, k):
    return pltpu.roll(values, LANES - TV - k, 1)


def spectral_scalars(modes_ref):
    row = lax.axis_index("row")
    rates = []
    for k in range(1, 4):
        total = jnp.float32(0.0)
        for j in range(3):
            mode = modes_ref[row, j]
            index = lax.rem(lax.rem(mode, 7) * k, 7)
            total = total + mode.astype(jnp.float32) * pick(SIN7, index)
        rates.append(total * jnp.float32(-time_scale * 2.0 * math.pi * 2.0 / 7.0))
    return rates


def goes_first():
    place = lax.axis_index("mesh")
    return lax.rem(place, 32) < 2


OUT_SHAPE = jax.ShapeDtypeStruct((TV, LINES, HALVES * LANES), F32)
FIELD = jax.ShapeDtypeStruct((HALVES * TV, LINES, LANES), F32)


def inner(pair_ref, flux, modes_ref, weights, state, inverse, mid, out, q0, inv, ghost, q1, q2, q3, paired, sems, out_sems):
    loads = []
    for h in range(HALVES):
        cut = pl.ds(h * LANES, LANES)
        loads.append(pltpu.make_async_copy(state.at[:, :, cut], q0.at[pl.ds(h * TV, TV)], sems.at[h]))
        loads.append(pltpu.make_async_copy(inverse.at[:, :, cut], inv.at[pl.ds(h * VV, VV)], sems.at[2 + h]))
    for copy in loads:
        copy.start()
    rates = spectral_scalars(modes_ref)
    start_line = lax.axis_index("mesh") * LINES
    for w in range(LINES):
        paired[pl.ds(w, 1), :] = mid[pl.ds(pair_ref[0, w] - start_line, 1), :]
    for w in range(0, LINES, 8):
        values = transfer(paired[pl.ds(w, 8), :], weights)
        for k in range(TV):
            ghost[k, pl.ds(w, 8), :] = to_lane_zero(values, k)
    for copy in loads:
        copy.wait()

    def section(src, dst, number, count, first, stop):
        weight = (number + 1.0) / SECTIONS
        scaled, spectral = section_weights(flux, rates, weight)

        def body(i, carry):
            r0 = jnp.minimum(first + i * 8, stop - 8)

            def emit(h, k, value):
                dst[h * TV + k, pl.ds(r0, 8), :] = value

            block_update(src, q0, inv, ghost, r0, scaled, spectral, weight, emit)
            return carry

        lax.fori_loop(0, count, body, 0)

    section(q0, q1, 0, 4, 2, LINES - 2)
    section(q1, q2, 1, 3, 4, LINES - 4)
    scaled, spectral = section_weights(flux, rates, 1.0)

    def results(i, h):
        at = pl.ds(pl.multiple_of(8 + i * 8, 8), 8)
        return pltpu.make_async_copy(
            q3.at[pl.ds(h * TV, TV), at, :], out.at[:, at, pl.ds(h * LANES, LANES)], out_sems.at[i, h]
        )

    def last(i, carry):
        r0 = pl.multiple_of(8 + i * 8, 8)

        def emit(h, k, value):
            q3[h * TV + k, pl.ds(r0, 8), :] = value

        block_update(q2, q0, inv, ghost, r0, scaled, spectral, 1.0, emit)
        for h in range(HALVES):
            results(i, h).start()
        return carry

    lax.fori_loop(0, 2, last, 0)
    for i in range(2):
        for h in range(HALVES):
            results(i, h).wait()


INNER_SHAPES = (
    OUT_SHAPE,
    FIELD,
    jax.ShapeDtypeStruct((HALVES * VV, LINES, LANES), F32),
    jax.ShapeDtypeStruct((TV, LINES, LANES), F32),
    FIELD,
    FIELD,
)
INNER_SCRATCH = [
    pltpu.VMEM((HALVES * TV, LINES, LANES), F32),
    pltpu.VMEM((LINES, LANES), F32),
    pltpu.SemaphoreType.DMA((4,)),
    pltpu.SemaphoreType.DMA((2, HALVES)),
]


def early_kernel(
    pair_ref, flux, modes_ref, delay_ref, state, inverse, mid,
    down, weights_ref, out, q0, inv, ghost, q1, q2, s_lo, i_lo, low_sems, q3, paired, sems, out_sems,
):
    lows = [
        pltpu.make_async_copy(state.at[:, pl.ds(0, 8), :], s_lo, low_sems.at[0]),
        pltpu.make_async_copy(inverse.at[:, pl.ds(0, 8), :], i_lo, low_sems.at[1]),
    ]
    for copy in lows:
        copy.start()
    start_line = lax.axis_index("mesh") * LINES
    weights = transfer_weights(modes_ref, delay_ref)
    for d in range(TIMES):
        weights_ref[d] = weights[d]
    for w in range(8):
        paired[pl.ds(w, 1), :] = mid[pl.ds(pair_ref[0, w] - start_line, 1), :]
    down[pl.ds(S_ROWS + I_ROWS, NEAR), :] = transfer(paired[pl.ds(0, 8), :], weights)[:NEAR, :]
    for copy in lows:
        copy.wait()
    pack_message(down, s_lo, i_lo, 0, 0)

    @pl.when(goes_first())
    def _():
        again = [weights_ref[d] for d in range(TIMES)]
        inner(
            pair_ref, flux, modes_ref, again, state, inverse, mid,
            out, q0, inv, ghost, q1, q2, q3, paired, sems, out_sems,
        )


def early(pairing, flux, modes, delay, state, inverse, mid):
    return pl.pallas_call(
        early_kernel,
        out_shape=(
            jax.ShapeDtypeStruct((MSG, LANES), F32),
            jax.ShapeDtypeStruct((TIMES, 8, LANES), F32),
        ) + INNER_SHAPES,
        in_specs=[SMEM] * 4 + [HBM] * 2 + [VMEM],
        out_specs=[VMEM, VMEM, HBM] + [VMEM] * 5,
        scratch_shapes=[
            pltpu.VMEM((TV, 8, HALVES * LANES), F32),
            pltpu.VMEM((VV, 8, HALVES * LANES), F32),
            pltpu.SemaphoreType.DMA((2,)),
        ] + INNER_SCRATCH,
        name="early",
        compiler_params=pltpu.CompilerParams(vmem_limit_bytes=10 << 20),
        cost_estimate=pl.CostEstimate(flops=30_000_000, bytes_accessed=3_000_000, transcendentals=0),
    )(pairing, flux, modes, delay, state, inverse, mid)


def late_kernel(
    pair_ref, flux, modes_ref, weights_ref, state, inverse, mid, _,
    out, q0, inv, ghost, q1, q2, q3, paired, sems, out_sems,
):
    @pl.when(jnp.logical_not(goes_first()))
    def _():
        weights = [weights_ref[d] for d in range(TIMES)]
        inner(
            pair_ref, flux, modes_ref, weights, state, inverse, mid,
            out, q0, inv, ghost, q1, q2, q3, paired, sems, out_sems,
        )


def late(pairing, flux, modes, weights, state, inverse, mid, out):
    return pl.pallas_call(
        late_kernel,
        out_shape=INNER_SHAPES,
        in_specs=[SMEM] * 3 + [VMEM] + [HBM] * 2 + [VMEM] + [HBM],
        out_specs=[HBM] + [VMEM] * 5,
        scratch_shapes=INNER_SCRATCH,
        input_output_aliases={7: 0},
        name="late",
        compiler_params=pltpu.CompilerParams(vmem_limit_bytes=10 << 20),
        cost_estimate=pl.CostEstimate(flops=30_000_000, bytes_accessed=3_000_000, transcendentals=0),
    )(pairing, flux, modes, weights, state, inverse, mid, out)


STRIP = 16


class Side:
    def __init__(self, low):
        if low:
            self.shift, self.halo, self.near = 22, 10, 10
            self.block, self.final, self.own = 6, 2, LINES - 8
            self.mine = (24, 8), (26, 2), (22, 6)
        else:
            self.shift, self.halo, self.near = -6, 0, 2
            self.block, self.final, self.own = 2, 6, 0
            self.mine = (0, 8), (4, 2), (4, 6)

    def rows(self, which):
        line, many = self.mine[which]
        return pl.ds(line - self.shift, many), pl.ds(line, many)


def edges_kernel(
    flux, modes_ref, weights_ref, got_dn, got_up, source, *rest,
):
    set_a, set_b, (_, out, *strips, sems) = rest[:5], rest[5:10], rest[10:]
    sides = []
    for at, (low, got) in enumerate(((True, got_dn), (False, got_up))):
        sides.append((Side(low), got, strips[6 * at : 6 * at + 6]))

    def bring(q0, inv, ghost, q1, q2):
        for side, _, (x0, x1, x2, iv, gh, x3) in sides:
            for which, dst, src in ((0, x0, q0), (0, iv, inv), (0, gh, ghost), (1, x1, q1), (2, x2, q2)):
                to, at = side.rows(which)
                for p in range(src.shape[0]):
                    dst[p, to, :] = src[p, at, :]

    first = goes_first()
    pl.when(first)(lambda: bring(*set_a))
    pl.when(jnp.logical_not(first))(lambda: bring(*set_b))
    lines = lax.broadcasted_iota(jnp.int32, (LINES, LANES), 0).astype(jnp.float32)
    chosen = []
    for j in range(NEAR):
        hit = lines == got_up[pl.ds(S_ROWS + I_ROWS + j, 1), :]
        chosen.append(jnp.sum(jnp.where(hit, source[...], 0.0), axis=0, keepdims=True))
    chosen = jnp.concatenate(chosen + [jnp.zeros((8 - NEAR, LANES), jnp.float32)], axis=0)
    chosen = transfer(chosen, [weights_ref[d] for d in range(TIMES)])[:NEAR, :]
    given = got_dn[pl.ds(S_ROWS + I_ROWS, NEAR), :]
    rates = spectral_scalars(modes_ref)
    for (side, got, (x0, x1, x2, iv, gh, x3)), values in zip(sides, (given, chosen)):
        for k in range(TV):
            gh[k, pl.ds(side.near, NEAR), :] = to_lane_zero(values, k)
        for p in range(HALVES * TV):
            x0[p, pl.ds(side.halo, DEEP), :] = got[pl.ds(p * DEEP, DEEP), :]
        for p in range(HALVES * VV):
            iv[p, pl.ds(side.near, NEAR), :] = got[pl.ds(S_ROWS + p * NEAR, NEAR), :]
    copies = []
    for at, (side, got, (x0, x1, x2, iv, gh, x3)) in enumerate(sides):
        for s, (src, dst) in enumerate(((x0, x1), (x1, x2))):
            weight = (s + 1.0) / SECTIONS
            scaled, spectral = section_weights(flux, rates, weight)

            def emit(h, k, value):
                dst[h * TV + k, pl.ds(side.block, 8), :] = value

            block_update(src, x0, iv, gh, side.block, scaled, spectral, weight, emit)
        scaled, spectral = section_weights(flux, rates, 1.0)

        def emit_last(h, k, value):
            x3[h * TV + k] = value

        block_update(x2, x0, iv, gh, side.final, scaled, spectral, 1.0, emit_last)
        for h in range(HALVES):
            copies.append(
                pltpu.make_async_copy(
                    x3.at[pl.ds(h * TV, TV)],
                    out.at[:, pl.ds(side.own, 8), pl.ds(h * LANES, LANES)],
                    sems.at[at, h],
                )
            )
            copies[-1].start()
    for copy in copies:
        copy.wait()


def edges(flux, modes, weights, got_dn, got_up, source, sets, out):
    return pl.pallas_call(
        edges_kernel,
        out_shape=OUT_SHAPE,
        in_specs=[SMEM] * 2 + [VMEM] * 14 + [HBM],
        out_specs=HBM,
        scratch_shapes=[
            pltpu.VMEM((HALVES * TV, STRIP, LANES), F32),
            pltpu.VMEM((HALVES * TV, STRIP, LANES), F32),
            pltpu.VMEM((HALVES * TV, STRIP, LANES), F32),
            pltpu.VMEM((HALVES * VV, STRIP, LANES), F32),
            pltpu.VMEM((TV, STRIP, LANES), F32),
            pltpu.VMEM((HALVES * TV, 8, LANES), F32),
        ] * 2 + [pltpu.SemaphoreType.DMA((2, HALVES))],
        input_output_aliases={16: 0},
        name="edges",
        compiler_params=pltpu.CompilerParams(vmem_limit_bytes=10 << 20),
        cost_estimate=pl.CostEstimate(flops=20_000_000, bytes_accessed=1_000_000, transcendentals=0),
    )(flux, modes, weights, got_dn, got_up, source, *sets, out)


def steps(state, inverse_blocks, flux_jacobian, harmonics, interface_delay, inflow, pairing):
    rows, devices = lax.axis_size("row"), lax.axis_size("mesh")
    local_state = state.reshape(TV, LINES, HALVES * LANES)
    local_inverse = inverse_blocks.reshape(VV, LINES, HALVES * LANES)
    local_state, local_inverse, flow, pairing = (
        pltpu.with_memory_space_constraint(array, pltpu.HBM)
        for array in (local_state, local_inverse, inflow.transpose(1, 0, 2), pairing)
    )
    up, outlet = pack(pairing, local_state, local_inverse, flow)
    onward = [(i, i + 1) for i in range(devices - 1)]
    back = [(j, i) for i, j in onward]

    def downstream(step):
        return [
            (r * devices + m, ((r + 1) % rows) * devices + m + step)
            for r in range(rows)
            for m in range(devices)
            if 0 <= m + step < devices
        ]

    mid = lax.ppermute(outlet, ("row", "mesh"), downstream(0))
    got_up = lax.ppermute(up, "mesh", onward)
    down, weights, out, *set_a = early(
        pairing, flux_jacobian, harmonics, interface_delay, local_state, local_inverse, mid
    )
    got_dn = lax.ppermute(down, "mesh", back)
    above = lax.ppermute(outlet, ("row", "mesh"), downstream(1))
    out, *set_b = late(pairing, flux_jacobian, harmonics, weights, local_state, local_inverse, mid, out)
    out = edges(flux_jacobian, harmonics, weights, got_dn, got_up, above, [*set_a, *set_b], out)
    return out.reshape(state.shape)


def solution(mesh):
    return jax.shard_map(
        steps,
        mesh=mesh,
        in_specs=(
            P("row", None, None, "mesh", None),
            P("row", None, None, "mesh", None),
            P("row", None, None),
            P(),
            P(),
            P(None, None, "mesh"),
            P("row", "mesh"),
        ),
        out_specs=P("row", None, None, "mesh", None),
        check_vma=False,
    )
```

```python
import functools
import math

import jax
import jax.numpy as jnp
from jax import lax
from jax.experimental import pallas as pl
from jax.experimental.pallas import tpu as pltpu
from jax.sharding import PartitionSpec as P


TIMES = 7
VARS = 5
TV = TIMES * VARS
VV = VARS * VARS
SECTIONS = 3
LANES = 128
HALVES = 2
DEEP = 6
NEAR = 4
LINES = 32
S_ROWS = HALVES * TV * DEEP
I_ROWS = HALVES * VV * NEAR
MSG = S_ROWS + I_ROWS + NEAR

nu_second = 0.25
nu_fourth = 0.03
time_scale = 0.05

COS7 = [math.cos(2.0 * math.pi * k / 7.0) for k in range(7)]
SIN7 = [math.sin(2.0 * math.pi * k / 7.0) for k in range(7)]


def pick(table, index):
    value = jnp.float32(table[0])
    for k in range(1, 7):
        value = jnp.where(index == k, jnp.float32(table[k]), value)
    return value


def pack_message(out, s_ref, i_ref, s_from, i_from):
    for h in range(HALVES):
        cut = pl.ds(h * LANES, LANES)
        for k in range(TV):
            out[pl.ds((h * TV + k) * DEEP, DEEP), :] = s_ref[k, pl.ds(s_from, DEEP), cut]
        for k in range(VV):
            out[pl.ds(S_ROWS + (h * VV + k) * NEAR, NEAR), :] = i_ref[k, pl.ds(i_from, NEAR), cut]


def outlet_kernel(state, inflow, outlet, last, flow, turned, sems):
    copy = pltpu.make_async_copy(state.at[:, :, pl.ds(LANES, LANES)], last, sems.at[0])
    copy.start()
    copy.wait()
    lane = lax.broadcasted_iota(jnp.int32, (LINES, LANES), 1)
    total = jnp.zeros((LINES, LANES), jnp.float32)
    for k in range(TV):
        total = jnp.where(lane == k, pltpu.roll(last[k], k + 1, 1), total)
    outlet[...] = total

    @pl.when(lax.axis_index("row") == lax.axis_size("row") - 1)
    def _():
        copy = pltpu.make_async_copy(inflow, flow, sems.at[1])
        copy.start()
        turned[...] = jnp.zeros((LANES, LANES), jnp.float32)
        copy.wait()
        for t in range(TIMES):
            for v in range(VARS):
                turned[pl.ds(t * VARS + v, 1), pl.ds(0, LINES)] = flow[v, pl.ds(t, 1), :]
        outlet[...] = jnp.transpose(turned[...])[:LINES, :]


F32 = jnp.float32
SMEM = pl.BlockSpec(memory_space=pltpu.SMEM)
VMEM = pl.BlockSpec(memory_space=pltpu.VMEM)
HBM = pl.BlockSpec(memory_space=pltpu.HBM)


def last_cells(state, inflow):
    return pl.pallas_call(
        outlet_kernel,
        out_shape=jax.ShapeDtypeStruct((LINES, LANES), F32),
        in_specs=[HBM, HBM],
        out_specs=VMEM,
        scratch_shapes=[
            pltpu.VMEM((TV, LINES, LANES), F32),
            pltpu.VMEM((VARS, TIMES, LINES), F32),
            pltpu.VMEM((LANES, LANES), F32),
            pltpu.SemaphoreType.DMA((2,)),
        ],
        name="outlet",
        compiler_params=pltpu.CompilerParams(vmem_limit_bytes=4 << 20),
        cost_estimate=pl.CostEstimate(flops=10000, bytes_accessed=600_000, transcendentals=0),
    )(state, inflow)


def section_weights(flux, spectral, weight):
    w = jnp.float32(weight)
    scaled = [[flux[0, a, b] * w for b in range(VARS)] for a in range(VARS)]
    return scaled, [d * w for d in spectral]


def block_update(src, base, inv, ghost, r0, scaled, spectral, weight, emit):
    first = lax.broadcasted_iota(jnp.int32, (8, LANES), 1) == 0
    centre_c = jnp.float32((2.0 * nu_second + 6.0 * nu_fourth) * weight)
    near_c = jnp.float32((-nu_second - 4.0 * nu_fourth) * weight)
    far_c = jnp.float32(nu_fourth * weight)
    for h in range(HALVES):
        for t in range(TIMES):
            diffs = []
            for v in range(VARS):
                k = t * VARS + v
                here = src[h * TV + k, pl.ds(r0, 8), :]
                turned = pltpu.roll(here, 1, 1)
                if h == 0:
                    edge = ghost[k, pl.ds(r0, 8), :]
                else:
                    edge = pltpu.roll(src[k, pl.ds(r0, 8), :], 1, 1)
                diffs.append(here - jnp.where(first, edge, turned))
            residual = []
            for v in range(VARS):
                p = h * TV + t * VARS + v
                here = src[p, pl.ds(r0, 8), :]
                near = src[p, pl.ds(r0 - 1, 8), :] + src[p, pl.ds(r0 + 1, 8), :]
                far = src[p, pl.ds(r0 - 2, 8), :] + src[p, pl.ds(r0 + 2, 8), :]
                value = centre_c * here + near_c * near + far_c * far
                for j in range(1, 4):
                    early = src[h * TV + ((t - j) % TIMES) * VARS + v, pl.ds(r0, 8), :]
                    late = src[h * TV + ((t + j) % TIMES) * VARS + v, pl.ds(r0, 8), :]
                    value = value + spectral[j - 1] * (early - late)
                for b in range(VARS):
                    value = value + scaled[v][b] * diffs[b]
                residual.append(value)
            for v in range(VARS):
                p = h * TV + t * VARS + v
                value = base[p, pl.ds(r0, 8), :]
                for b in range(VARS):
                    value = value - inv[h * VV + v * VARS + b, pl.ds(r0, 8), :] * residual[b]
                emit(h, t * VARS + v, value)


def transfer_weights(modes_ref, delay_ref):
    row = lax.axis_index("row")
    upstream = jnp.maximum(row - 1, 0)
    delay = delay_ref[row]
    waves = []
    for j in range(3):
        mode = modes_ref[upstream, j]
        phase = jnp.full((8, LANES), mode.astype(jnp.float32) * delay, jnp.float32)
        phase = (phase - jnp.round(phase)) * jnp.float32(2.0 * math.pi)
        waves.append((lax.rem(mode, 7), jnp.cos(phase), jnp.sin(phase)))
    weights = []
    for d in range(TIMES):
        weight = jnp.full((8, LANES), 1.0 / 7.0, jnp.float32)
        for rest, cosine, sine in waves:
            index = lax.rem(rest * d, 7)
            weight = weight + jnp.float32(2.0 / 7.0) * (cosine * pick(COS7, index) - sine * pick(SIN7, index))
        weights.append(weight)
    return weights


def transfer(paired, weights):
    doubled = paired + pltpu.roll(paired, TV, 1)
    total = weights[0] * doubled
    for d in range(1, TIMES):
        total = total + weights[d] * pltpu.roll(doubled, VARS * d, 1)
    return total


def to_lane_zero(values, k):
    return pltpu.roll(values, LANES - TV - k, 1)


def spectral_scalars(modes_ref):
    row = lax.axis_index("row")
    rates = []
    for k in range(1, 4):
        total = jnp.float32(0.0)
        for j in range(3):
            mode = modes_ref[row, j]
            index = lax.rem(lax.rem(mode, 7) * k, 7)
            total = total + mode.astype(jnp.float32) * pick(SIN7, index)
        rates.append(total * jnp.float32(-time_scale * 2.0 * math.pi * 2.0 / 7.0))
    return rates


def goes_first():
    place = lax.axis_index("mesh")
    return lax.rem(place, 32) < 2


OUT_SHAPE = jax.ShapeDtypeStruct((TV, LINES, HALVES * LANES), F32)
FIELD = jax.ShapeDtypeStruct((HALVES * TV, LINES, LANES), F32)


def inner(pair_ref, flux, modes_ref, weights, state, inverse, mid, out, q0, inv, ghost, q1, q2, q3, paired, sems, out_sems):
    loads = []
    for h in range(HALVES):
        cut = pl.ds(h * LANES, LANES)
        loads.append(pltpu.make_async_copy(state.at[:, :, cut], q0.at[pl.ds(h * TV, TV)], sems.at[h]))
        loads.append(pltpu.make_async_copy(inverse.at[:, :, cut], inv.at[pl.ds(h * VV, VV)], sems.at[2 + h]))
    for copy in loads:
        copy.start()
    rates = spectral_scalars(modes_ref)
    start_line = lax.axis_index("mesh") * LINES
    for w in range(LINES):
        paired[pl.ds(w, 1), :] = mid[pl.ds(pair_ref[0, w] - start_line, 1), :]
    for w in range(0, LINES, 8):
        values = transfer(paired[pl.ds(w, 8), :], weights)
        for k in range(TV):
            ghost[k, pl.ds(w, 8), :] = to_lane_zero(values, k)
    for copy in loads:
        copy.wait()

    def section(src, dst, number, count, first, stop):
        weight = (number + 1.0) / SECTIONS
        scaled, spectral = section_weights(flux, rates, weight)

        def body(i, carry):
            r0 = jnp.minimum(first + i * 8, stop - 8)

            def emit(h, k, value):
                dst[h * TV + k, pl.ds(r0, 8), :] = value

            block_update(src, q0, inv, ghost, r0, scaled, spectral, weight, emit)
            return carry

        lax.fori_loop(0, count, body, 0)

    section(q0, q1, 0, 4, 2, LINES - 2)
    section(q1, q2, 1, 3, 4, LINES - 4)
    scaled, spectral = section_weights(flux, rates, 1.0)

    def results(i, h):
        at = pl.ds(pl.multiple_of(8 + i * 8, 8), 8)
        return pltpu.make_async_copy(
            q3.at[pl.ds(h * TV, TV), at, :], out.at[:, at, pl.ds(h * LANES, LANES)], out_sems.at[i, h]
        )

    def last(i, carry):
        r0 = pl.multiple_of(8 + i * 8, 8)

        def emit(h, k, value):
            q3[h * TV + k, pl.ds(r0, 8), :] = value

        block_update(q2, q0, inv, ghost, r0, scaled, spectral, 1.0, emit)
        for h in range(HALVES):
            results(i, h).start()
        return carry

    lax.fori_loop(0, 2, last, 0)
    for i in range(2):
        for h in range(HALVES):
            results(i, h).wait()


INNER_SHAPES = (
    OUT_SHAPE,
    FIELD,
    jax.ShapeDtypeStruct((HALVES * VV, LINES, LANES), F32),
    jax.ShapeDtypeStruct((TV, LINES, LANES), F32),
    FIELD,
    FIELD,
)
INNER_SCRATCH = [
    pltpu.VMEM((HALVES * TV, LINES, LANES), F32),
    pltpu.VMEM((LINES, LANES), F32),
    pltpu.SemaphoreType.DMA((4,)),
    pltpu.SemaphoreType.DMA((2, HALVES)),
]


def early_kernel(
    pair_ref, flux, modes_ref, delay_ref, state, inverse, mid,
    up, down, weights_ref, out, q0, inv, ghost, q1, q2,
    s_hi, i_hi, s_lo, i_lo, tile_sems, q3, paired, sems, out_sems,
):
    top = pl.ds(LINES - 8, 8)
    tiles = [
        pltpu.make_async_copy(state.at[:, top, :], s_hi, tile_sems.at[0]),
        pltpu.make_async_copy(inverse.at[:, top, :], i_hi, tile_sems.at[1]),
        pltpu.make_async_copy(state.at[:, pl.ds(0, 8), :], s_lo, tile_sems.at[2]),
        pltpu.make_async_copy(inverse.at[:, pl.ds(0, 8), :], i_lo, tile_sems.at[3]),
    ]
    for copy in tiles:
        copy.start()
    start_line = lax.axis_index("mesh") * LINES
    weights = transfer_weights(modes_ref, delay_ref)
    for d in range(TIMES):
        weights_ref[d] = weights[d]
    for j in range(NEAR):
        paired[pl.ds(j, 1), :] = mid[pl.ds(pair_ref[0, j] - start_line, 1), :]
        paired[pl.ds(8 + j, 1), :] = mid[pl.ds(pair_ref[0, LINES - NEAR + j] - start_line, 1), :]
    down[pl.ds(S_ROWS + I_ROWS, NEAR), :] = transfer(paired[pl.ds(0, 8), :], weights)[:NEAR, :]
    up[pl.ds(S_ROWS + I_ROWS, NEAR), :] = transfer(paired[pl.ds(8, 8), :], weights)[:NEAR, :]
    for copy in tiles:
        copy.wait()
    pack_message(up, s_hi, i_hi, 8 - DEEP, 8 - NEAR)
    pack_message(down, s_lo, i_lo, 0, 0)

    @pl.when(goes_first())
    def _():
        again = [weights_ref[d] for d in range(TIMES)]
        inner(
            pair_ref, flux, modes_ref, again, state, inverse, mid,
            out, q0, inv, ghost, q1, q2, q3, paired, sems, out_sems,
        )


def early(pairing, flux, modes, delay, state, inverse, mid):
    return pl.pallas_call(
        early_kernel,
        out_shape=(
            jax.ShapeDtypeStruct((MSG, LANES), F32),
            jax.ShapeDtypeStruct((MSG, LANES), F32),
            jax.ShapeDtypeStruct((TIMES, 8, LANES), F32),
        ) + INNER_SHAPES,
        in_specs=[SMEM] * 4 + [HBM] * 2 + [VMEM],
        out_specs=[VMEM, VMEM, VMEM, HBM] + [VMEM] * 5,
        scratch_shapes=[
            pltpu.VMEM((TV, 8, HALVES * LANES), F32),
            pltpu.VMEM((VV, 8, HALVES * LANES), F32),
            pltpu.VMEM((TV, 8, HALVES * LANES), F32),
            pltpu.VMEM((VV, 8, HALVES * LANES), F32),
            pltpu.SemaphoreType.DMA((4,)),
        ] + INNER_SCRATCH,
        name="early",
        compiler_params=pltpu.CompilerParams(vmem_limit_bytes=10 << 20),
        cost_estimate=pl.CostEstimate(flops=30_000_000, bytes_accessed=3_000_000, transcendentals=0),
    )(pairing, flux, modes, delay, state, inverse, mid)


def late_kernel(
    pair_ref, flux, modes_ref, weights_ref, state, inverse, mid, _,
    out, q0, inv, ghost, q1, q2, q3, paired, sems, out_sems,
):
    @pl.when(jnp.logical_not(goes_first()))
    def _():
        weights = [weights_ref[d] for d in range(TIMES)]
        inner(
            pair_ref, flux, modes_ref, weights, state, inverse, mid,
            out, q0, inv, ghost, q1, q2, q3, paired, sems, out_sems,
        )


def late(pairing, flux, modes, weights, state, inverse, mid, out):
    return pl.pallas_call(
        late_kernel,
        out_shape=INNER_SHAPES,
        in_specs=[SMEM] * 3 + [VMEM] + [HBM] * 2 + [VMEM] + [HBM],
        out_specs=[HBM] + [VMEM] * 5,
        scratch_shapes=INNER_SCRATCH,
        input_output_aliases={7: 0},
        name="late",
        compiler_params=pltpu.CompilerParams(vmem_limit_bytes=10 << 20),
        cost_estimate=pl.CostEstimate(flops=30_000_000, bytes_accessed=3_000_000, transcendentals=0),
    )(pairing, flux, modes, weights, state, inverse, mid, out)


STRIP = 16


class Side:
    def __init__(self, low):
        if low:
            self.shift, self.halo, self.near = 22, 10, 10
            self.block, self.final, self.own = 6, 2, LINES - 8
            self.mine = (24, 8), (26, 2), (22, 6)
        else:
            self.shift, self.halo, self.near = -6, 0, 2
            self.block, self.final, self.own = 2, 6, 0
            self.mine = (0, 8), (4, 2), (4, 6)

    def rows(self, which):
        line, many = self.mine[which]
        return pl.ds(line - self.shift, many), pl.ds(line, many)


def edge_kernel(low, flux, modes_ref, got, *rest):
    set_a, set_b, (_, out, x0, x1, x2, iv, gh, x3, sems) = rest[:5], rest[5:10], rest[10:]
    side = Side(low)

    def bring(q0, inv, ghost, q1, q2):
        for which, dst, src in ((0, x0, q0), (0, iv, inv), (0, gh, ghost), (1, x1, q1), (2, x2, q2)):
            to, at = side.rows(which)
            for p in range(src.shape[0]):
                dst[p, to, :] = src[p, at, :]

    first = goes_first()
    pl.when(first)(lambda: bring(*set_a))
    pl.when(jnp.logical_not(first))(lambda: bring(*set_b))
    values = got[pl.ds(S_ROWS + I_ROWS, NEAR), :]
    rates = spectral_scalars(modes_ref)
    for k in range(TV):
        gh[k, pl.ds(side.near, NEAR), :] = to_lane_zero(values, k)
    for p in range(HALVES * TV):
        x0[p, pl.ds(side.halo, DEEP), :] = got[pl.ds(p * DEEP, DEEP), :]
    for p in range(HALVES * VV):
        iv[p, pl.ds(side.near, NEAR), :] = got[pl.ds(S_ROWS + p * NEAR, NEAR), :]
    for s, (src, dst) in enumerate(((x0, x1), (x1, x2))):
        weight = (s + 1.0) / SECTIONS
        scaled, spectral = section_weights(flux, rates, weight)

        def emit(h, k, value):
            dst[h * TV + k, pl.ds(side.block, 8), :] = value

        block_update(src, x0, iv, gh, side.block, scaled, spectral, weight, emit)
    scaled, spectral = section_weights(flux, rates, 1.0)

    def emit_last(h, k, value):
        x3[h * TV + k] = value

    block_update(x2, x0, iv, gh, side.final, scaled, spectral, 1.0, emit_last)
    copies = [
        pltpu.make_async_copy(
            x3.at[pl.ds(h * TV, TV)], out.at[:, pl.ds(side.own, 8), pl.ds(h * LANES, LANES)], sems.at[h]
        )
        for h in range(HALVES)
    ]
    for copy in copies:
        copy.start()
    for copy in copies:
        copy.wait()


def edge(low, flux, modes, got, sets, out):
    return pl.pallas_call(
        functools.partial(edge_kernel, low),
        out_shape=OUT_SHAPE,
        in_specs=[SMEM] * 2 + [VMEM] * 11 + [HBM],
        out_specs=HBM,
        scratch_shapes=[
            pltpu.VMEM((HALVES * TV, STRIP, LANES), F32),
            pltpu.VMEM((HALVES * TV, STRIP, LANES), F32),
            pltpu.VMEM((HALVES * TV, STRIP, LANES), F32),
            pltpu.VMEM((HALVES * VV, STRIP, LANES), F32),
            pltpu.VMEM((TV, STRIP, LANES), F32),
            pltpu.VMEM((HALVES * TV, 8, LANES), F32),
            pltpu.SemaphoreType.DMA((HALVES,)),
        ],
        input_output_aliases={13: 0},
        name="low" if low else "high",
        compiler_params=pltpu.CompilerParams(vmem_limit_bytes=6 << 20),
        cost_estimate=pl.CostEstimate(flops=10_000_000, bytes_accessed=1_000_000, transcendentals=0),
    )(flux, modes, got, *sets, out)


def steps(state, inverse_blocks, flux_jacobian, harmonics, interface_delay, inflow, pairing):
    rows, devices = lax.axis_size("row"), lax.axis_size("mesh")
    local_state = state.reshape(TV, LINES, HALVES * LANES)
    local_inverse = inverse_blocks.reshape(VV, LINES, HALVES * LANES)
    local_state, local_inverse, flow, pairing = (
        pltpu.with_memory_space_constraint(array, pltpu.HBM)
        for array in (local_state, local_inverse, inflow.transpose(1, 0, 2), pairing)
    )
    outlet = last_cells(local_state, flow)
    onward = [(i, i + 1) for i in range(devices - 1)]
    back = [(j, i) for i, j in onward]

    def downstream(step):
        return [
            (r * devices + m, ((r + 1) % rows) * devices + m + step)
            for r in range(rows)
            for m in range(devices)
            if 0 <= m + step < devices
        ]

    mid = lax.ppermute(outlet, ("row", "mesh"), downstream(0))
    up, down, weights, out, *set_a = early(
        pairing, flux_jacobian, harmonics, interface_delay, local_state, local_inverse, mid
    )
    got_up = lax.ppermute(up, "mesh", onward)
    got_dn = lax.ppermute(down, "mesh", back)
    out, *set_b = late(pairing, flux_jacobian, harmonics, weights, local_state, local_inverse, mid, out)
    sets = [*set_a, *set_b]
    out = edge(False, flux_jacobian, harmonics, got_up, sets, out)
    out = edge(True, flux_jacobian, harmonics, got_dn, sets, out)
    return out.reshape(state.shape)


def solution(mesh):
    return jax.shard_map(
        steps,
        mesh=mesh,
        in_specs=(
            P("row", None, None, "mesh", None),
            P("row", None, None, "mesh", None),
            P("row", None, None),
            P(),
            P(),
            P(None, None, "mesh"),
            P("row", "mesh"),
        ),
        out_specs=P("row", None, None, "mesh", None),
        check_vma=False,
    )
```
